32 devices in a mesh: tok: 8 (over y, x, core), own: 4 (over z).
Axes of the slice: x: 2, y: 2, z: 4, core: 2. Of those that a mesh axis runs over, the one named last changes fastest.
Arguments:
- expert_ids: int32 [5, 8, 262144], P(None, None, ('tok', 'own')), may hold values from 0 to 383, as said below
- shard_length: int32 [32], P(('tok', 'own')), may hold values from 2048 to 8192
Outputs:
- lift: float32 [4, 384, 384], P(None, 'own')
The draws below stay inside these ranges and needn't reach their ends.
Inputs may be any that keep to these rules, and one draw needn't show every extreme that they name: For each layer and token slot, expert_ids names 8 different experts.
All inputs are finite; a program needn't handle non-finite values.
Results may differ from the reference program's by a relative error of at most 0.0003.
Values sent between devices are 32-bit elements; how exact they have to be, the bound alone decides.
A program may use at most 64 MiB of HBM per device.

```python
import math
import jax
import jax.numpy as jnp
from jax import lax

E = 384
K = 8
LAYERS = 5
TOK_DEV = 8192
PAIRS = 4
TOKENS = 262144
DEVICES = 32


def draw_expert_ids(key, part):
    rows = math.gcd(TOKENS, 8192)
    blocks = TOKENS // rows
    experts = jnp.arange(E, dtype=jnp.int32)

    def one_layer(layer):
        layer_key = jax.random.fold_in(key, 7001 + layer)
        favour = jax.random.randint(jax.random.fold_in(layer_key, 1), (E,), 0, 2 ** 19, dtype=jnp.int32)
        order = jax.random.permutation(jax.random.fold_in(layer_key, 2), experts)
        banned = jnp.any(experts[:, None] == order[None, :3], axis=1)

        def one_block(index):
            block_key = jax.random.fold_in(layer_key, 100 + index)
            noise = jax.random.randint(block_key, (rows, E), 0, 2 ** 20, dtype=jnp.int32)
            score = (noise + favour[None, :]) * E + experts[None, :]
            score = jnp.where(banned[None, :], -1 - experts[None, :], score)
            return lax.top_k(score, K)[1].astype(jnp.int32)
        picked = lax.map(one_block, jnp.arange(blocks, dtype=jnp.int32))
        return jnp.transpose(picked.reshape(TOKENS, K), (1, 0))
    return lax.map(one_layer, jnp.arange(LAYERS, dtype=jnp.int32))


def set_ends(drawn, own_key, smallest, top_value):
    index_at = [jax.random.randint(jax.random.fold_in(own_key, axis), (), 0, length) for axis, length in enumerate(drawn.shape)]
    main_axis = drawn.shape.index(max(drawn.shape))
    neighbour = index_at[:main_axis] + [(index_at[main_axis] + 1) % drawn.shape[main_axis]] + index_at[main_axis + 1:]
    return drawn.at[tuple(index_at)].set(smallest).at[tuple(neighbour)].set(top_value)


def setup_inputs(seed: int = 0) -> dict:
    seeds = jax.random.split(jax.random.key(seed), 3)
    expert_ids = draw_expert_ids(jax.random.fold_in(seeds[2], 71), 0)
    shard_length = set_ends(jax.random.randint(seeds[1], (DEVICES,), TOK_DEV // 4, TOK_DEV + 1), jax.random.fold_in(seeds[1], 1), TOK_DEV // 4, TOK_DEV).astype(jnp.int32)
    return {"expert_ids": expert_ids, "shard_length": shard_length}


def reference(expert_ids, shard_length):
    routes = jnp.transpose(expert_ids, (0, 2, 1))
    position = jnp.arange(TOKENS, dtype=jnp.int32)
    owner = position // TOK_DEV
    live = (position - owner * TOK_DEV < shard_length[owner]).astype(jnp.float32)
    total = jnp.sum(shard_length.astype(jnp.float32))
    weights = jnp.broadcast_to(live[:, None], (TOKENS, K))
    counts = jnp.stack([jnp.zeros((E,), jnp.float32).at[routes[l]].add(weights) for l in range(LAYERS)])
    pair_weights = jnp.broadcast_to(live[:, None, None], (TOKENS, K, K))
    tiles = []
    for p in range(PAIRS):
        index = routes[p][:, :, None] * E + routes[p + 1][:, None, :]
        flat = jnp.zeros((E * E,), jnp.float32).at[index].add(pair_weights)
        tiles.append(flat.reshape(E, E))
    pair_counts = jnp.stack(tiles)
    product = counts[:-1, :, None] * counts[1:, None, :]
    return pair_counts * total / jnp.maximum(product, 1.0)
```

```python
import functools

import jax
import jax.numpy as jnp
from jax import lax
from jax.experimental import pallas as pl
from jax.experimental.pallas import tpu as pltpu
from jax.sharding import PartitionSpec as P

E = 384
LANES = 128
ROWS = 8
COLS = E // LANES
WORDS = E // 32
HOT = jnp.bfloat16
MESH = pl.DeviceIdType.MESH


def halvings(bits, tiles):
    kept = []
    for _ in range(bits):
        split = tiles % 2 == 0 and (tiles // 2) % COLS == 0
        tiles = tiles // 2 if split else tiles
        kept.append((tiles, split))
    return kept


def kernel(bits, owners, kept, limit_ref, ids_ref, out_ref, hot, macc, acc, first, *rest):
    nst = len(kept)
    stage_in = rest[:nst]
    zsend, zrecv, gathered, csem, ssem, zsem, gsem = rest[nst:]
    layers, chosen, slots = ids_ref.shape
    pairs = layers - 1
    nslot = pairs // 2
    share = acc.shape[2]
    piece = kept[-1][0] if kept else share
    pieces = share // piece

    tok = lax.axis_index("tok")
    own = lax.axis_index("own")
    core = tok % 2
    bit = []
    delta = []
    for i in range(nst):
        bit.append((tok // (2 << i)) % 2)
        delta.append((1 - 2 * bit[i]) * (2 << i))
    if nst >= 2:
        b0, b1, d0, d1 = bit[0], bit[1], delta[0], delta[1]
        bit[0] = b0 * (1 - core) + b1 * core
        bit[1] = b1 * (1 - core) + b0 * core
        delta[0] = d0 * (1 - core) + d1 * core
        delta[1] = d1 * (1 - core) + d0 * core
    partner = [tok + d for d in delta]
    mate = tok + 1 - 2 * core

    barrier = pltpu.get_barrier_semaphore()
    for other in [mate] + partner:
        pl.semaphore_signal(barrier, inc=1, device_id={"tok": other}, device_id_type=MESH)
    for d in range(1, owners):
        pl.semaphore_signal(
            barrier, inc=1, device_id={"own": (own + d) % owners}, device_id_type=MESH
        )

    limit = limit_ref[0]
    step = 512
    row = lax.broadcasted_iota(jnp.int32, (32, step), 0)
    mask = jnp.left_shift(jnp.int32(1), row)

    def build(layer):
        def chunk(index, _):
            start = pl.multiple_of(index * step, step)
            x = ids_ref[layer, :, pl.ds(start, step)]
            at = start + lax.broadcasted_iota(jnp.int32, x.shape, 1)
            high = jnp.where(at < limit, jnp.right_shift(x, 5), WORDS)
            value = jnp.left_shift(jnp.int32(1), jnp.bitwise_and(x, 31))
            for w in range(WORDS):
                word = jnp.sum(jnp.where(high == w, value, 0), axis=0, keepdims=True)
                on = jnp.bitwise_and(jnp.broadcast_to(word, mask.shape), mask) != 0
                hot[layer, pl.ds(32 * w, 32), pl.ds(start, step)] = jnp.where(
                    on, 1.0, 0.0
                ).astype(HOT)
            return 0

        lax.fori_loop(0, slots // step, chunk, 0)

    depth = 1024

    def matmul(pair):
        macc[...] = jnp.zeros_like(macc)

        def chunk(index, _):
            at = pl.ds(pl.multiple_of(index * depth, depth), depth)
            macc[...] += lax.dot_general(
                hot[pair, :, at],
                hot[pair + 1, :, at],
                (((1,), (1,)), ((), ())),
                preferred_element_type=jnp.float32,
            )
            return 0

        lax.fori_loop(0, slots // depth, chunk, 0)
        groups = share // COLS
        for g in range(E // ROWS):
            for b in range(COLS):
                acc[pair, g // groups, (g % groups) * COLS + b] = macc[
                    g * ROWS : (g + 1) * ROWS, b * LANES : (b + 1) * LANES
                ]

    def mine(s):
        return 2 * s + core

    def theirs(s):
        return 2 * s + 1 - core

    def core_copy(s):
        return pltpu.make_async_remote_copy(
            src_ref=acc.at[theirs(s)],
            dst_ref=first.at[s],
            send_sem=csem.at[0, s],
            recv_sem=csem.at[1, s],
            device_id={"tok": mate},
            device_id_type=MESH,
        )

    def offset(i):
        at = 0
        for j in range(i):
            if kept[j][1]:
                at = at + bit[j] * kept[j][0]
        return at

    def stage_copy(s, i):
        size, split = kept[i]
        at = offset(i) + ((1 - bit[i]) * size if split else 0)
        return pltpu.make_async_remote_copy(
            src_ref=acc.at[mine(s), :, pl.ds(at, size)],
            dst_ref=stage_in[i].at[s],
            send_sem=ssem.at[0, s, i],
            recv_sem=ssem.at[1, s, i],
            device_id={"tok": partner[i]},
            device_id_type=MESH,
        )

    def stage_add(s, i):
        size = kept[i][0]
        at = pl.ds(offset(i + 1), size)
        for o in range(owners):
            acc[mine(s), o, at] = acc[mine(s), o, at] + stage_in[i][s, o]

    def z_copy(s, d):
        return pltpu.make_async_remote_copy(
            src_ref=zsend.at[s, (own + d) % owners],
            dst_ref=zrecv.at[s, d - 1],
            send_sem=zsem.at[0, s, d],
            recv_sem=zsem.at[1, s, d],
            device_id={"own": (own + d) % owners},
            device_id_type=MESH,
        )

    def z_send(s):
        at = pl.ds(offset(nst), piece)
        part = acc[mine(s), :, at]
        sums = []
        for b in range(COLS):
            total = jnp.zeros((ROWS, LANES), jnp.float32)
            for o in range(owners):
                for t in range(b, piece, COLS):
                    total = total + part[o, t]
            sums.append(jnp.sum(total, axis=0, keepdims=True))
        sums.append(jnp.zeros((ROWS - COLS, LANES), jnp.float32))
        extra = jnp.concatenate(sums, axis=0)
        for o in range(owners):
            zsend[s, o, pl.ds(0, piece)] = part[o]
            zsend[s, o, piece] = extra
        for d in range(1, owners):
            z_copy(s, d).start()

    def place(i):
        at, span = 0, pieces
        for j in range(i + 1):
            if kept[j][1]:
                span = span // 2
                at = at + bit[j] * span
        return at, span

    def z_sum(s):
        total = zsend[s, own]
        for d in range(1, owners):
            total = total + zrecv[s, d - 1]
        where, _ = place(nst - 1)
        gathered[mine(s), where] = total

    def gather_copy(s, i):
        at, span = place(i)
        there = gathered.at[mine(s), pl.ds(at, span)]
        return pltpu.make_async_remote_copy(
            src_ref=there,
            dst_ref=there,
            send_sem=gsem.at[0, s, i + 1],
            recv_sem=gsem.at[1, s, i + 1],
            device_id={"tok": partner[i]},
            device_id_type=MESH,
        )

    def mate_copy(s):
        return pltpu.make_async_remote_copy(
            src_ref=gathered.at[mine(s)],
            dst_ref=gathered.at[mine(s)],
            send_sem=gsem.at[0, s, 0],
            recv_sem=gsem.at[1, s, 0],
            device_id={"tok": mate},
            device_id_type=MESH,
        )

    def lift(pair):
        second = jnp.zeros((ROWS, LANES), jnp.float32)
        for q in range(pieces):
            second = second + gathered[pair, q, piece]
        second = second / chosen
        total = jnp.sum(jnp.sum(second, axis=1, keepdims=True), axis=0, keepdims=True) / chosen
        for g in range(share // COLS):
            tiles = []
            for b in range(COLS):
                t = g * COLS + b
                tiles.append(gathered[pair, t // piece, t % piece])
            mass = jnp.sum(tiles[0] + tiles[1] + tiles[2], axis=1, keepdims=True) / chosen
            for b in range(COLS):
                product = mass * second[b : b + 1, :]
                out_ref[pair, pl.ds(g * ROWS, ROWS), pl.ds(b * LANES, LANES)] = (
                    tiles[b] * total / jnp.maximum(product, 1.0)
                )

    gathers = [i for i in reversed(range(nst)) if kept[i][1]]

    def stages(s):
        core_copy(s).wait()
        acc[mine(s)] = acc[mine(s)] + first[s]
        for i in range(nst):
            stage_copy(s, i).start()
            yield
            stage_copy(s, i).wait()
            stage_add(s, i)
        z_send(s)
        yield
        for d in range(1, owners):
            z_copy(s, d).wait()
        z_sum(s)
        for i in gathers:
            gather_copy(s, i).start()
            yield
            gather_copy(s, i).wait()
        mate_copy(s).start()
        yield
        mate_copy(s).wait()
        lift(2 * s)
        lift(2 * s + 1)

    def advance(run):
        try:
            next(run)
            return True
        except StopIteration:
            return False

    build(0)
    build(1)
    build(2)
    pl.semaphore_wait(barrier, 1 + nst + owners - 1)
    matmul(theirs(0))
    core_copy(0).start()
    matmul(mine(0))
    runs = [stages(0)]
    advance(runs[0])
    for s in range(1, nslot):
        build(2 * s + 1)
        advance(runs[-1])
        build(2 * s + 2)
        advance(runs[-1])
        matmul(theirs(s))
        core_copy(s).start()
        advance(runs[-1])
        matmul(mine(s))
        runs.append(stages(s))
        advance(runs[-1])
    live = list(runs)
    while live:
        live = [run for run in live if advance(run)]


def shards(expert_ids, shard_length):
    layers, chosen, slots = expert_ids.shape
    toks = lax.axis_size("tok")
    owners = lax.axis_size("own")
    bits = toks.bit_length() - 2
    share = E // owners // ROWS * COLS
    kept = halvings(bits, share)
    piece = kept[-1][0]
    pieces = share // piece
    pairs = layers - 1
    nslot = pairs // 2
    tile = (ROWS, LANES)
    f32 = jnp.float32
    dma = pltpu.SemaphoreType.DMA
    scratch = [
        pltpu.VMEM((layers, E, slots), HOT),
        pltpu.VMEM((E, E), f32),
        pltpu.VMEM((pairs, owners, share) + tile, f32),
        pltpu.VMEM((nslot, owners, share) + tile, f32),
    ]
    scratch += [pltpu.VMEM((nslot, owners, size) + tile, f32) for size, _ in kept]
    scratch += [
        pltpu.VMEM((nslot, owners, piece + 1) + tile, f32),
        pltpu.VMEM((nslot, owners - 1, piece + 1) + tile, f32),
        pltpu.VMEM((pairs, pieces, piece + 1) + tile, f32),
        dma((2, nslot)),
        dma((2, nslot, bits)),
        dma((2, nslot, owners)),
        dma((2, nslot, bits + 1)),
    ]
    return pl.pallas_call(
        functools.partial(kernel, bits, owners, kept),
        out_shape=jax.ShapeDtypeStruct((pairs, E // owners, E), f32),
        in_specs=[
            pl.BlockSpec(memory_space=pltpu.SMEM),
            pl.BlockSpec(memory_space=pltpu.VMEM),
        ],
        out_specs=pl.BlockSpec(memory_space=pltpu.VMEM),
        scratch_shapes=scratch,
        compiler_params=pltpu.CompilerParams(
            collective_id=0, has_side_effects=True, vmem_limit_bytes=60 * 2**20
        ),
    )(shard_length, expert_ids)


def solution(mesh):
    placed = (P(None, None, ("tok", "own")), P(("tok", "own")))
    return jax.shard_map(
        shards, mesh=mesh, in_specs=placed, out_specs=P(None, "own", None), check_vma=False
    )
```

```python
import functools

import jax
import jax.numpy as jnp
from jax import lax
from jax.experimental import pallas as pl
from jax.experimental.pallas import tpu as pltpu
from jax.sharding import PartitionSpec as P

E = 384
LANES = 128
ROWS = 8
COLS = E // LANES
WORDS = E // 32
HOT = jnp.float8_e4m3fn
MESH = pl.DeviceIdType.MESH


def halvings(bits, tiles):
    kept = []
    for _ in range(bits):
        split = tiles % 2 == 0 and (tiles // 2) % COLS == 0
        tiles = tiles // 2 if split else tiles
        kept.append((tiles, split))
    return kept


def kernel(bits, owners, kept, limit_ref, ids_ref, out_ref, *rest):
    layers, chosen, slots = ids_ref.shape
    hot, (macc, acc, first), rest = rest[:layers], rest[layers : layers + 3], rest[layers + 3 :]
    nst = len(kept)
    stage_in = rest[:nst]
    zsend, zrecv, gathered, csem, ssem, zsem, gsem = rest[nst:]
    pairs = layers - 1
    nslot = pairs // 2
    share = acc.shape[2]
    piece = kept[-1][0] if kept else share
    pieces = share // piece

    tok = lax.axis_index("tok")
    own = lax.axis_index("own")
    core = tok % 2
    bit = []
    delta = []
    for i in range(nst):
        bit.append((tok // (2 << i)) % 2)
        delta.append((1 - 2 * bit[i]) * (2 << i))
    if nst >= 2:
        b0, b1, d0, d1 = bit[0], bit[1], delta[0], delta[1]
        bit[0] = b0 * (1 - core) + b1 * core
        bit[1] = b1 * (1 - core) + b0 * core
        delta[0] = d0 * (1 - core) + d1 * core
        delta[1] = d1 * (1 - core) + d0 * core
    partner = [tok + d for d in delta]
    mate = tok + 1 - 2 * core

    barrier = pltpu.get_barrier_semaphore()
    for other in [mate] + partner:
        pl.semaphore_signal(barrier, inc=1, device_id={"tok": other}, device_id_type=MESH)
    for d in range(1, owners):
        pl.semaphore_signal(
            barrier, inc=1, device_id={"own": (own + d) % owners}, device_id_type=MESH
        )

    limit = limit_ref[0]
    step = 512
    row = lax.broadcasted_iota(jnp.int32, (32, step), 0)
    mask = jnp.left_shift(jnp.int32(1), row % 8).astype(jnp.int8)

    def build(layer, start):
        x = ids_ref[layer, :, pl.ds(start, step)]
        at = start + lax.broadcasted_iota(jnp.int32, x.shape, 1)
        high = jnp.where(at < limit, jnp.right_shift(x, 5), WORDS)
        value = jnp.left_shift(jnp.int32(1), jnp.bitwise_and(x, 31))
        for w in range(WORDS):
            word = jnp.sum(jnp.where(high == w, value, 0), axis=0, keepdims=True)
            bytes4 = jnp.concatenate(
                [jnp.broadcast_to(jnp.right_shift(word, 8 * j), (8, step)) for j in range(4)],
                axis=0,
            ).astype(jnp.int8)
            on = jnp.bitwise_and(bytes4, mask) != 0
            hot[layer][pl.ds(32 * w, 32), pl.ds(start, step)] = jnp.where(
                on, jnp.ones((32, step), HOT), jnp.zeros((32, step), HOT)
            )

    depth = min(slots, 2048)
    groups = share // COLS

    def work(layers_now, pair):
        if pair is not None:
            macc[...] = jnp.zeros_like(macc)

        def chunk(index, _):
            start = pl.multiple_of(index * depth, depth)
            if pair is not None:
                at = pl.ds(start, depth)
                macc[...] += lax.dot_general(
                    hot[pair][:, at],
                    hot[pair + 1][:, at],
                    (((1,), (1,)), ((), ())),
                    preferred_element_type=jnp.float32,
                )
            for layer in layers_now:
                for piece_at in range(0, depth, step):
                    build(layer, start + piece_at)
            return 0

        lax.fori_loop(0, slots // depth, chunk, 0)
        if pair is not None:
            for g in range(E // ROWS):
                for b in range(COLS):
                    acc[pair, g // groups, (g % groups) * COLS + b] = macc[
                        g * ROWS : (g + 1) * ROWS, b * LANES : (b + 1) * LANES
                    ]

    def mine(s):
        return 2 * s + core

    def theirs(s):
        return 2 * s + 1 - core

    def core_copy(s):
        return pltpu.make_async_remote_copy(
            src_ref=acc.at[theirs(s)],
            dst_ref=first.at[s],
            send_sem=csem.at[0, s],
            recv_sem=csem.at[1, s],
            device_id={"tok": mate},
            device_id_type=MESH,
        )

    def offset(i):
        at = 0
        for j in range(i):
            if kept[j][1]:
                at = at + bit[j] * kept[j][0]
        return at

    def stage_copy(s, i):
        size, split = kept[i]
        at = offset(i) + ((1 - bit[i]) * size if split else 0)
        return pltpu.make_async_remote_copy(
            src_ref=acc.at[mine(s), :, pl.ds(at, size)],
            dst_ref=stage_in[i].at[s],
            send_sem=ssem.at[0, s, i],
            recv_sem=ssem.at[1, s, i],
            device_id={"tok": partner[i]},
            device_id_type=MESH,
        )

    def stage_add(s, i):
        size = kept[i][0]
        at = pl.ds(offset(i + 1), size)
        for o in range(owners):
            acc[mine(s), o, at] = acc[mine(s), o, at] + stage_in[i][s, o]

    def z_copy(s, d):
        return pltpu.make_async_remote_copy(
            src_ref=zsend.at[s, (own + d) % owners],
            dst_ref=zrecv.at[s, d - 1],
            send_sem=zsem.at[0, s, d],
            recv_sem=zsem.at[1, s, d],
            device_id={"own": (own + d) % owners},
            device_id_type=MESH,
        )

    def z_send(s):
        at = pl.ds(offset(nst), piece)
        part = acc[mine(s), :, at]
        sums = []
        for b in range(COLS):
            total = jnp.zeros((ROWS, LANES), jnp.float32)
            for o in range(owners):
                for t in range(b, piece, COLS):
                    total = total + part[o, t]
            sums.append(jnp.sum(total, axis=0, keepdims=True))
        sums.append(jnp.zeros((ROWS - COLS, LANES), jnp.float32))
        extra = jnp.concatenate(sums, axis=0)
        for o in range(owners):
            zsend[s, o, pl.ds(0, piece)] = part[o]
            zsend[s, o, piece] = extra
        for d in range(1, owners):
            z_copy(s, d).start()

    def place(i):
        at, span = 0, pieces
        for j in range(i + 1):
            if kept[j][1]:
                span = span // 2
                at = at + bit[j] * span
        return at, span

    def z_sum(s):
        total = zsend[s, own]
        for d in range(1, owners):
            total = total + zrecv[s, d - 1]
        where, _ = place(nst - 1)
        gathered[mine(s), where] = total

    def gather_copy(s, i):
        at, span = place(i)
        there = gathered.at[mine(s), pl.ds(at, span)]
        return pltpu.make_async_remote_copy(
            src_ref=there,
            dst_ref=there,
            send_sem=gsem.at[0, s, i + 1],
            recv_sem=gsem.at[1, s, i + 1],
            device_id={"tok": partner[i]},
            device_id_type=MESH,
        )

    def mate_copy(s):
        return pltpu.make_async_remote_copy(
            src_ref=gathered.at[mine(s)],
            dst_ref=gathered.at[mine(s)],
            send_sem=gsem.at[0, s, 0],
            recv_sem=gsem.at[1, s, 0],
            device_id={"tok": mate},
            device_id_type=MESH,
        )

    def lift(pair):
        second = jnp.zeros((ROWS, LANES), jnp.float32)
        for q in range(pieces):
            second = second + gathered[pair, q, piece]
        second = second / chosen
        total = jnp.sum(jnp.sum(second, axis=1, keepdims=True), axis=0, keepdims=True) / chosen
        for g in range(share // COLS):
            tiles = []
            for b in range(COLS):
                t = g * COLS + b
                tiles.append(gathered[pair, t // piece, t % piece])
            mass = jnp.sum(tiles[0] + tiles[1] + tiles[2], axis=1, keepdims=True) / chosen
            for b in range(COLS):
                product = mass * second[b : b + 1, :]
                out_ref[pair, pl.ds(g * ROWS, ROWS), pl.ds(b * LANES, LANES)] = (
                    tiles[b] * total / jnp.maximum(product, 1.0)
                )

    gathers = [i for i in reversed(range(nst)) if kept[i][1]]

    def stages(s):
        core_copy(s).wait()
        acc[mine(s)] = acc[mine(s)] + first[s]
        for i in range(nst):
            stage_copy(s, i).start()
            yield
            stage_copy(s, i).wait()
            stage_add(s, i)
        z_send(s)
        yield
        for d in range(1, owners):
            z_copy(s, d).wait()
        z_sum(s)
        for i in gathers:
            gather_copy(s, i).start()
            yield
            gather_copy(s, i).wait()
        mate_copy(s).start()
        yield
        mate_copy(s).wait()
        lift(2 * s)
        lift(2 * s + 1)

    def advance(run):
        try:
            next(run)
            return True
        except StopIteration:
            return False

    work((0,), None)
    work((1,), None)
    runs = []
    for p in range(pairs):
        work((p + 2,) if p + 2 < layers else (), p)
        if p == 0:
            pl.semaphore_wait(barrier, 1 + nst + owners - 1)
        for run in runs:
            advance(run)
        if p % 2 == 1:
            core_copy(p // 2).start()
            runs.append(stages(p // 2))
            advance(runs[-1])
    live = list(runs)
    while live:
        live = [run for run in live if advance(run)]


def shards(expert_ids, shard_length):
    layers, chosen, slots = expert_ids.shape
    toks = lax.axis_size("tok")
    owners = lax.axis_size("own")
    bits = toks.bit_length() - 2
    share = E // owners // ROWS * COLS
    kept = halvings(bits, share)
    piece = kept[-1][0]
    pieces = share // piece
    pairs = layers - 1
    nslot = pairs // 2
    tile = (ROWS, LANES)
    f32 = jnp.float32
    dma = pltpu.SemaphoreType.DMA
    scratch = [pltpu.VMEM((E, slots), HOT)] * layers
    scratch += [
        pltpu.VMEM((E, E), f32),
        pltpu.VMEM((pairs, owners, share) + tile, f32),
        pltpu.VMEM((nslot, owners, share) + tile, f32),
    ]
    scratch += [pltpu.VMEM((nslot, owners, size) + tile, f32) for size, _ in kept]
    scratch += [
        pltpu.VMEM((nslot, owners, piece + 1) + tile, f32),
        pltpu.VMEM((nslot, owners - 1, piece + 1) + tile, f32),
        pltpu.VMEM((pairs, pieces, piece + 1) + tile, f32),
        dma((2, nslot)),
        dma((2, nslot, bits)),
        dma((2, nslot, owners)),
        dma((2, nslot, bits + 1)),
    ]
    return pl.pallas_call(
        functools.partial(kernel, bits, owners, kept),
        out_shape=jax.ShapeDtypeStruct((pairs, E // owners, E), f32),
        in_specs=[
            pl.BlockSpec(memory_space=pltpu.SMEM),
            pl.BlockSpec(memory_space=pltpu.VMEM),
        ],
        out_specs=pl.BlockSpec(memory_space=pltpu.VMEM),
        scratch_shapes=scratch,
        compiler_params=pltpu.CompilerParams(
            collective_id=0, has_side_effects=True, vmem_limit_bytes=60 * 2**20
        ),
    )(shard_length, expert_ids)


def solution(mesh):
    placed = (P(None, None, ("tok", "own")), P(("tok", "own")))
    return jax.shard_map(
        shards, mesh=mesh, in_specs=placed, out_specs=P(None, "own", None), check_vma=False
    )
```

```python
import functools

import jax
import jax.numpy as jnp
from jax import lax
from jax.experimental import pallas as pl
from jax.experimental.pallas import tpu as pltpu
from jax.sharding import PartitionSpec as P

E = 384
LANES = 128
ROWS = 8
COLS = E // LANES
WORDS = E // 32
HOT = jnp.float8_e4m3fn
MESH = pl.DeviceIdType.MESH


def halvings(bits, tiles):
    kept = []
    for _ in range(bits):
        split = tiles % 2 == 0 and (tiles // 2) % COLS == 0
        tiles = tiles // 2 if split else tiles
        kept.append((tiles, split))
    return kept


def kernel(bits, owners, kept, limit_ref, ids_ref, out_ref, *rest):
    layers, chosen, slots = ids_ref.shape
    hot, (macc, acc, first), rest = rest[:layers], rest[layers : layers + 3], rest[layers + 3 :]
    nst = len(kept)
    stage_in = rest[:nst]
    zsend, zrecv, gathered, xsum, xin, xz, xcol = rest[nst : nst + 7]
    csem, ssem, zsem, gsem, xsem, xzsem = rest[nst + 7 :]
    pairs = layers - 1
    nslot = pairs // 2
    share = acc.shape[2]
    piece = kept[-1][0] if kept else share
    pieces = share // piece

    tok = lax.axis_index("tok")
    own = lax.axis_index("own")
    core = tok % 2
    bit = []
    delta = []
    for i in range(nst):
        bit.append((tok // (2 << i)) % 2)
        delta.append((1 - 2 * bit[i]) * (2 << i))
    if nst >= 2:
        b0, b1, d0, d1 = bit[0], bit[1], delta[0], delta[1]
        bit[0] = b0 * (1 - core) + b1 * core
        bit[1] = b1 * (1 - core) + b0 * core
        delta[0] = d0 * (1 - core) + d1 * core
        delta[1] = d1 * (1 - core) + d0 * core
    partner = [tok + d for d in delta]
    mate = tok + 1 - 2 * core

    split = [i for i in range(nst) if kept[i][1]]
    peers = {}
    for code in range(1, 2 ** len(split)):
        peers[code] = tok + sum(delta[i] for n, i in enumerate(split) if (code >> n) % 2)
    greet = [mate] + list(peers.values())
    greet += [partner[i] for i in range(nst) if i not in split]

    barrier = pltpu.get_barrier_semaphore()
    for other in greet:
        pl.semaphore_signal(barrier, inc=1, device_id={"tok": other}, device_id_type=MESH)
    for d in range(1, owners):
        pl.semaphore_signal(
            barrier, inc=1, device_id={"own": (own + d) % owners}, device_id_type=MESH
        )
    turn = sorted(range(1, owners), key=lambda d: -min(d, owners - d)) + [0]

    def to(d):
        return (own + d) % owners

    limit = limit_ref[0]
    step = 512
    row = lax.broadcasted_iota(jnp.int32, (32, step), 0)
    mask = jnp.left_shift(jnp.int32(1), row % 8).astype(jnp.int8)

    def build(layer, start):
        x = ids_ref[layer, :, pl.ds(start, step)]
        at = start + lax.broadcasted_iota(jnp.int32, x.shape, 1)
        high = jnp.where(at < limit, jnp.right_shift(x, 5), WORDS)
        value = jnp.left_shift(jnp.int32(1), jnp.bitwise_and(x, 31))
        for w in range(WORDS):
            word = jnp.sum(jnp.where(high == w, value, 0), axis=0, keepdims=True)
            bytes4 = jnp.concatenate(
                [jnp.broadcast_to(jnp.right_shift(word, 8 * j), (8, step)) for j in range(4)],
                axis=0,
            ).astype(jnp.int8)
            on = jnp.bitwise_and(bytes4, mask) != 0
            hot[layer][pl.ds(32 * w, 32), pl.ds(start, step)] = jnp.where(
                on, jnp.ones((32, step), HOT), jnp.zeros((32, step), HOT)
            )

    depth = min(slots, 2048)
    groups = share // COLS

    def work(layers_now, pair):
        if pair is not None:
            macc[...] = jnp.zeros_like(macc)

        def chunk(index, _):
            start = pl.multiple_of(index * depth, depth)
            if pair is not None:
                at = pl.ds(start, depth)
                macc[...] += lax.dot_general(
                    hot[pair][:, at],
                    hot[pair + 1][:, at],
                    (((1,), (1,)), ((), ())),
                    preferred_element_type=jnp.float32,
                )
            for layer in layers_now:
                for piece_at in range(0, depth, step):
                    build(layer, start + piece_at)
            return 0

        lax.fori_loop(0, slots // depth, chunk, 0)
        if pair is not None:
            for g in range(E // ROWS):
                for b in range(COLS):
                    acc[pair, g // groups, (g % groups) * COLS + b] = macc[
                        g * ROWS : (g + 1) * ROWS, b * LANES : (b + 1) * LANES
                    ]

    def mine(s):
        return 2 * s + core

    def theirs(s):
        return 2 * s + 1 - core

    def core_copy(s, d):
        return pltpu.make_async_remote_copy(
            src_ref=acc.at[theirs(s), to(d)],
            dst_ref=first.at[s, to(d)],
            send_sem=csem.at[0, s, d],
            recv_sem=csem.at[1, s, d],
            device_id={"tok": mate},
            device_id_type=MESH,
        )

    def offset(i):
        at = 0
        for j in range(i):
            if kept[j][1]:
                at = at + bit[j] * kept[j][0]
        return at

    def stage_copy(s, i, d):
        size, halves = kept[i]
        at = offset(i) + ((1 - bit[i]) * size if halves else 0)
        return pltpu.make_async_remote_copy(
            src_ref=acc.at[mine(s), to(d), pl.ds(at, size)],
            dst_ref=stage_in[i].at[s, to(d)],
            send_sem=ssem.at[0, s, i, d],
            recv_sem=ssem.at[1, s, i, d],
            device_id={"tok": partner[i]},
            device_id_type=MESH,
        )

    def stage_add(s, i, d):
        at = pl.ds(offset(i + 1), kept[i][0])
        acc[mine(s), to(d), at] = acc[mine(s), to(d), at] + stage_in[i][s, to(d)]

    def z_copy(s, d):
        return pltpu.make_async_remote_copy(
            src_ref=zsend.at[s, d],
            dst_ref=zrecv.at[s, d - 1],
            send_sem=zsem.at[0, s, d],
            recv_sem=zsem.at[1, s, d],
            device_id={"own": to(d)},
            device_id_type=MESH,
        )

    def column_sums(s):
        sums = []
        for b in range(COLS):
            total = jnp.zeros((ROWS, LANES), jnp.float32)
            for o in range(owners):
                for t in range(b, share, COLS):
                    total = total + acc[mine(s), o, t]
            sums.append(jnp.sum(total, axis=0, keepdims=True))
        sums.append(jnp.zeros((ROWS - COLS, LANES), jnp.float32))
        return jnp.concatenate(sums, axis=0)

    def sums_copy(s, i):
        return pltpu.make_async_remote_copy(
            src_ref=xsum.at[s, i],
            dst_ref=xin.at[s, i],
            send_sem=xsem.at[0, s, i],
            recv_sem=xsem.at[1, s, i],
            device_id={"tok": partner[i]},
            device_id_type=MESH,
        )

    def sums_z_copy(s, d):
        return pltpu.make_async_remote_copy(
            src_ref=xsum.at[s, nst],
            dst_ref=xz.at[s, d - 1],
            send_sem=xzsem.at[0, s, d],
            recv_sem=xzsem.at[1, s, d],
            device_id={"own": to(d)},
            device_id_type=MESH,
        )

    def sums_mate_copy(s):
        return pltpu.make_async_remote_copy(
            src_ref=xcol.at[mine(s)],
            dst_ref=xcol.at[mine(s)],
            send_sem=xzsem.at[0, s, 0],
            recv_sem=xzsem.at[1, s, 0],
            device_id={"tok": mate},
            device_id_type=MESH,
        )

    def place(code):
        at, span = 0, pieces
        for n, i in enumerate(split):
            span = span // 2
            held = 1 - bit[i] if (code >> n) % 2 else bit[i]
            at = at + held * span
        return at

    def gather_copy(s, code):
        there = gathered.at[mine(s), place(0)]
        return pltpu.make_async_remote_copy(
            src_ref=there,
            dst_ref=there,
            send_sem=gsem.at[0, s, 0, code],
            recv_sem=gsem.at[1, s, 0, code],
            device_id={"tok": peers[code]},
            device_id_type=MESH,
        )

    def mate_copy(s, code):
        there = gathered.at[mine(s), place(code)]
        return pltpu.make_async_remote_copy(
            src_ref=there,
            dst_ref=there,
            send_sem=gsem.at[0, s, 1, code],
            recv_sem=gsem.at[1, s, 1, code],
            device_id={"tok": mate},
            device_id_type=MESH,
        )

    def lift(pair):
        second = xcol[pair] / chosen
        total = jnp.sum(jnp.sum(second, axis=1, keepdims=True), axis=0, keepdims=True) / chosen
        for g in range(share // COLS):
            tiles = []
            for b in range(COLS):
                t = g * COLS + b
                tiles.append(gathered[pair, t // piece, t % piece])
            mass = jnp.sum(tiles[0] + tiles[1] + tiles[2], axis=1, keepdims=True) / chosen
            for b in range(COLS):
                product = mass * second[b : b + 1, :]
                out_ref[pair, pl.ds(g * ROWS, ROWS), pl.ds(b * LANES, LANES)] = (
                    tiles[b] * total / jnp.maximum(product, 1.0)
                )

    def stages(s):
        for d in turn:
            core_copy(s, d).wait()
            acc[mine(s), to(d)] = acc[mine(s), to(d)] + first[s, to(d)]
            stage_copy(s, 0, d).start()
        xsum[s, 0] = column_sums(s)
        sums_copy(s, 0).start()
        yield
        for i in range(nst):
            sums_copy(s, i).wait()
            xsum[s, i + 1] = xsum[s, i] + xin[s, i]
            if i + 1 < nst:
                sums_copy(s, i + 1).start()
            else:
                for d in turn[:-1]:
                    sums_z_copy(s, d).start()
            for d in turn:
                stage_copy(s, i, d).wait()
                stage_add(s, i, d)
                if i + 1 < nst:
                    stage_copy(s, i + 1, d).start()
                    continue
                zsend[s, d] = acc[mine(s), to(d), pl.ds(offset(nst), piece)]
                if d:
                    z_copy(s, d).start()
            yield
        column = xsum[s, nst]
        for d in turn[:-1]:
            sums_z_copy(s, d).wait()
            column = column + xz[s, d - 1]
        xcol[mine(s)] = column
        sums_mate_copy(s).start()
        total = zsend[s, 0]
        for d in turn[:-1]:
            z_copy(s, d).wait()
            total = total + zrecv[s, d - 1]
        gathered[mine(s), place(0)] = total
        for code in reversed(peers):
            gather_copy(s, code).start()
        mate_copy(s, 0).start()
        yield
        for code in peers:
            gather_copy(s, code).wait()
            mate_copy(s, code).start()
        lift(mine(s))
        sums_mate_copy(s).wait()
        for code in [0] + list(peers):
            mate_copy(s, code).wait()
        lift(theirs(s))

    def advance(run):
        try:
            next(run)
            return True
        except StopIteration:
            return False

    work((0,), None)
    work((1,), None)
    runs = []
    for p in range(pairs):
        work((p + 2,) if p + 2 < layers else (), p)
        if p == 0:
            pl.semaphore_wait(barrier, len(greet) + owners - 1)
        if p % 2 == 1:
            for d in turn:
                core_copy(p // 2, d).start()
            for run in runs:
                advance(run)
            runs.append(stages(p // 2))
            advance(runs[-1])
    live = list(runs)
    while live:
        live = [run for run in live if advance(run)]


def shards(expert_ids, shard_length):
    layers, chosen, slots = expert_ids.shape
    toks = lax.axis_size("tok")
    owners = lax.axis_size("own")
    bits = toks.bit_length() - 2
    share = E // owners // ROWS * COLS
    kept = halvings(bits, share)
    piece = kept[-1][0]
    pieces = share // piece
    pairs = layers - 1
    nslot = pairs // 2
    tile = (ROWS, LANES)
    f32 = jnp.float32
    dma = pltpu.SemaphoreType.DMA
    scratch = [pltpu.VMEM((E, slots), HOT)] * layers
    scratch += [
        pltpu.VMEM((E, E), f32),
        pltpu.VMEM((pairs, owners, share) + tile, f32),
        pltpu.VMEM((nslot, owners, share) + tile, f32),
    ]
    scratch += [pltpu.VMEM((nslot, owners, size) + tile, f32) for size, _ in kept]
    scratch += [
        pltpu.VMEM((nslot, owners, piece) + tile, f32),
        pltpu.VMEM((nslot, owners - 1, piece) + tile, f32),
        pltpu.VMEM((pairs, pieces, piece) + tile, f32),
        pltpu.VMEM((nslot, bits + 1) + tile, f32),
        pltpu.VMEM((nslot, bits) + tile, f32),
        pltpu.VMEM((nslot, owners - 1) + tile, f32),
        pltpu.VMEM((pairs,) + tile, f32),
        dma((2, nslot, owners)),
        dma((2, nslot, bits, owners)),
        dma((2, nslot, owners)),
        dma((2, nslot, 2, pieces)),
        dma((2, nslot, bits)),
        dma((2, nslot, owners)),
    ]
    return pl.pallas_call(
        functools.partial(kernel, bits, owners, kept),
        out_shape=jax.ShapeDtypeStruct((pairs, E // owners, E), f32),
        in_specs=[
            pl.BlockSpec(memory_space=pltpu.SMEM),
            pl.BlockSpec(memory_space=pltpu.VMEM),
        ],
        out_specs=pl.BlockSpec(memory_space=pltpu.VMEM),
        scratch_shapes=scratch,
        compiler_params=pltpu.CompilerParams(
            collective_id=0, has_side_effects=True, vmem_limit_bytes=60 * 2**20
        ),
    )(shard_length, expert_ids)


def solution(mesh):
    placed = (P(None, None, ("tok", "own")), P(("tok", "own")))
    return jax.shard_map(
        shards, mesh=mesh, in_specs=placed, out_specs=P(None, "own", None), check_vma=False
    )
```

```python
import functools

import jax
import jax.numpy as jnp
from jax import lax
from jax.experimental import pallas as pl
from jax.experimental.pallas import tpu as pltpu
from jax.sharding import PartitionSpec as P

E = 384
LANES = 128
ROWS = 8
COLS = E // LANES
WORDS = E // 32
HOT = jnp.float8_e4m3fn
MESH = pl.DeviceIdType.MESH


def halvings(bits, tiles):
    kept = []
    for _ in range(bits):
        split = tiles % 2 == 0 and (tiles // 2) % COLS == 0
        tiles = tiles // 2 if split else tiles
        kept.append((tiles, split))
    return kept


def kernel(bits, owners, kept, limit_ref, ids_ref, out_ref, *rest):
    layers, chosen, slots = ids_ref.shape
    hot, (macc, acc, first), rest = rest[:layers], rest[layers : layers + 3], rest[layers + 3 :]
    nst = len(kept)
    stage_in = rest[:nst]
    zsend, zrecv, gathered, xsum, xin, xz, xcol = rest[nst : nst + 7]
    csem, ssem, zsem, gsem, xsem, xzsem = rest[nst + 7 :]
    pairs = layers - 1
    nslot = pairs // 2
    share = acc.shape[2]
    piece = kept[-1][0] if kept else share
    pieces = share // piece

    tok = lax.axis_index("tok")
    own = lax.axis_index("own")
    core = tok % 2
    bit = []
    delta = []
    for i in range(nst):
        bit.append((tok // (2 << i)) % 2)
        delta.append((1 - 2 * bit[i]) * (2 << i))
    if nst >= 2:
        b0, b1, d0, d1 = bit[0], bit[1], delta[0], delta[1]
        bit[0] = b0 * (1 - core) + b1 * core
        bit[1] = b1 * (1 - core) + b0 * core
        delta[0] = d0 * (1 - core) + d1 * core
        delta[1] = d1 * (1 - core) + d0 * core
    partner = [tok + d for d in delta]
    mate = tok + 1 - 2 * core

    split = [i for i in range(nst) if kept[i][1]]
    peers = {}
    for code in range(1, 2 ** len(split)):
        peers[code] = tok + sum(delta[i] for n, i in enumerate(split) if (code >> n) % 2)
    greet = [mate] + list(peers.values())
    greet += [partner[i] for i in range(nst) if i not in split]

    barrier = pltpu.get_barrier_semaphore()
    for other in greet:
        pl.semaphore_signal(barrier, inc=1, device_id={"tok": other}, device_id_type=MESH)
    for d in range(1, owners):
        pl.semaphore_signal(
            barrier, inc=1, device_id={"own": (own + d) % owners}, device_id_type=MESH
        )
    turn = sorted(range(1, owners), key=lambda d: -min(d, owners - d)) + [0]

    def to(d):
        return (own + d) % owners

    limit = limit_ref[0]
    step = 512
    row = lax.broadcasted_iota(jnp.int32, (32, step), 0)
    mask = jnp.left_shift(jnp.int32(1), row % 8).astype(jnp.int8)

    def build(layer, start):
        x = ids_ref[layer, :, pl.ds(start, step)]
        at = start + lax.broadcasted_iota(jnp.int32, x.shape, 1)
        high = jnp.where(at < limit, jnp.right_shift(x, 5), WORDS)
        value = jnp.left_shift(jnp.int32(1), jnp.bitwise_and(x, 31))
        for w in range(WORDS):
            word = jnp.sum(jnp.where(high == w, value, 0), axis=0, keepdims=True)
            bytes4 = jnp.concatenate(
                [jnp.broadcast_to(jnp.right_shift(word, 8 * j), (8, step)) for j in range(4)],
                axis=0,
            ).astype(jnp.int8)
            on = jnp.bitwise_and(bytes4, mask) != 0
            hot[layer][pl.ds(32 * w, 32), pl.ds(start, step)] = jnp.where(
                on, jnp.ones((32, step), HOT), jnp.zeros((32, step), HOT)
            )

    depth = min(slots, 2048)
    groups = share // COLS

    def work(layers_now, pair):
        if pair is not None:
            macc[...] = jnp.zeros_like(macc)

        def chunk(index, _):
            start = pl.multiple_of(index * depth, depth)
            if pair is not None:
                at = pl.ds(start, depth)
                macc[...] += lax.dot_general(
                    hot[pair][:, at],
                    hot[pair + 1][:, at],
                    (((1,), (1,)), ((), ())),
                    preferred_element_type=jnp.float32,
                )
            for layer in layers_now:
                for piece_at in range(0, depth, step):
                    build(layer, start + piece_at)
            return 0

        lax.fori_loop(0, slots // depth, chunk, 0)
        if pair is not None:
            for g in range(E // ROWS):
                for b in range(COLS):
                    acc[pair, g // groups, (g % groups) * COLS + b] = macc[
                        g * ROWS : (g + 1) * ROWS, b * LANES : (b + 1) * LANES
                    ]

    def mine(s):
        return 2 * s + core

    def theirs(s):
        return 2 * s + 1 - core

    def core_copy(s, d):
        return pltpu.make_async_remote_copy(
            src_ref=acc.at[theirs(s), to(d)],
            dst_ref=first.at[s, to(d)],
            send_sem=csem.at[0, s, d],
            recv_sem=csem.at[1, s, d],
            device_id={"tok": mate},
            device_id_type=MESH,
        )

    def offset(i):
        at = 0
        for j in range(i):
            if kept[j][1]:
                at = at + bit[j] * kept[j][0]
        return at

    def stage_copy(s, i, d):
        size, halves = kept[i]
        at = offset(i) + ((1 - bit[i]) * size if halves else 0)
        return pltpu.make_async_remote_copy(
            src_ref=acc.at[mine(s), to(d), pl.ds(at, size)],
            dst_ref=stage_in[i].at[s, to(d)],
            send_sem=ssem.at[0, s, i, d],
            recv_sem=ssem.at[1, s, i, d],
            device_id={"tok": partner[i]},
            device_id_type=MESH,
        )

    def stage_add(s, i, d):
        at = pl.ds(offset(i + 1), kept[i][0])
        acc[mine(s), to(d), at] = acc[mine(s), to(d), at] + stage_in[i][s, to(d)]

    def z_copy(s, d):
        return pltpu.make_async_remote_copy(
            src_ref=zsend.at[s, d],
            dst_ref=zrecv.at[s, d - 1],
            send_sem=zsem.at[0, s, d],
            recv_sem=zsem.at[1, s, d],
            device_id={"own": to(d)},
            device_id_type=MESH,
        )

    def column_sums(s):
        sums = []
        for b in range(COLS):
            total = jnp.zeros((ROWS, LANES), jnp.float32)
            for o in range(owners):
                for t in range(b, share, COLS):
                    total = total + acc[mine(s), o, t]
            sums.append(jnp.sum(total, axis=0, keepdims=True))
        sums.append(jnp.zeros((ROWS - COLS, LANES), jnp.float32))
        return jnp.concatenate(sums, axis=0)

    def sums_copy(s, i):
        return pltpu.make_async_remote_copy(
            src_ref=xsum.at[s, i],
            dst_ref=xin.at[s, i],
            send_sem=xsem.at[0, s, i],
            recv_sem=xsem.at[1, s, i],
            device_id={"tok": partner[i]},
            device_id_type=MESH,
        )

    def sums_z_copy(s, d):
        return pltpu.make_async_remote_copy(
            src_ref=xsum.at[s, nst],
            dst_ref=xz.at[s, d - 1],
            send_sem=xzsem.at[0, s, d],
            recv_sem=xzsem.at[1, s, d],
            device_id={"own": to(d)},
            device_id_type=MESH,
        )

    def sums_mate_copy(s):
        return pltpu.make_async_remote_copy(
            src_ref=xcol.at[mine(s)],
            dst_ref=xcol.at[mine(s)],
            send_sem=xzsem.at[0, s, 0],
            recv_sem=xzsem.at[1, s, 0],
            device_id={"tok": mate},
            device_id_type=MESH,
        )

    def place(code):
        at, span = 0, pieces
        for n, i in enumerate(split):
            span = span // 2
            held = 1 - bit[i] if (code >> n) % 2 else bit[i]
            at = at + held * span
        return at

    def gather_copy(s, code):
        there = gathered.at[mine(s), place(0)]
        return pltpu.make_async_remote_copy(
            src_ref=there,
            dst_ref=there,
            send_sem=gsem.at[0, s, 0, code],
            recv_sem=gsem.at[1, s, 0, code],
            device_id={"tok": peers[code]},
            device_id_type=MESH,
        )

    def mate_copy(s, code):
        there = gathered.at[mine(s), place(code)]
        return pltpu.make_async_remote_copy(
            src_ref=there,
            dst_ref=there,
            send_sem=gsem.at[0, s, 1, code],
            recv_sem=gsem.at[1, s, 1, code],
            device_id={"tok": mate},
            device_id_type=MESH,
        )

    def lift(pair):
        second = xcol[pair] / chosen
        total = jnp.sum(jnp.sum(second, axis=1, keepdims=True), axis=0, keepdims=True) / chosen
        for g in range(share // COLS):
            tiles = []
            for b in range(COLS):
                t = g * COLS + b
                tiles.append(gathered[pair, t // piece, t % piece])
            mass = jnp.sum(tiles[0] + tiles[1] + tiles[2], axis=1, keepdims=True) / chosen
            for b in range(COLS):
                product = mass * second[b : b + 1, :]
                out_ref[pair, pl.ds(g * ROWS, ROWS), pl.ds(b * LANES, LANES)] = (
                    tiles[b] * total / jnp.maximum(product, 1.0)
                )

    def stages(s):
        for d in turn:
            core_copy(s, d).wait()
            acc[mine(s), to(d)] = acc[mine(s), to(d)] + first[s, to(d)]
            stage_copy(s, 0, d).start()
        xsum[s, 0] = column_sums(s)
        sums_copy(s, 0).start()
        yield
        for i in range(nst):
            sums_copy(s, i).wait()
            xsum[s, i + 1] = xsum[s, i] + xin[s, i]
            if i + 1 < nst:
                sums_copy(s, i + 1).start()
            else:
                for d in turn[:-1]:
                    sums_z_copy(s, d).start()
            for d in turn:
                stage_copy(s, i, d).wait()
                stage_add(s, i, d)
                if i + 1 < nst:
                    stage_copy(s, i + 1, d).start()
                    continue
                zsend[s, d] = acc[mine(s), to(d), pl.ds(offset(nst), piece)]
                if d:
                    z_copy(s, d).start()
            yield
        column = xsum[s, nst]
        for d in turn[:-1]:
            sums_z_copy(s, d).wait()
            column = column + xz[s, d - 1]
        xcol[mine(s)] = column
        sums_mate_copy(s).start()
        total = zsend[s, 0]
        for d in turn[:-1]:
            z_copy(s, d).wait()
            total = total + zrecv[s, d - 1]
        gathered[mine(s), place(0)] = total
        for code in reversed(peers):
            gather_copy(s, code).start()
        mate_copy(s, 0).start()
        yield
        for code in peers:
            gather_copy(s, code).wait()
            mate_copy(s, code).start()
        lift(mine(s))
        sums_mate_copy(s).wait()
        for code in [0] + list(peers):
            mate_copy(s, code).wait()
        lift(theirs(s))

    def advance(run):
        try:
            next(run)
            return True
        except StopIteration:
            return False

    work((0,), None)
    work((1,), None)
    runs = []
    for p in range(pairs):
        work((p + 2,) if p + 2 < layers else (), p)
        if p == 0:
            pl.semaphore_wait(barrier, len(greet) + owners - 1)
        if p % 2 == 1:
            for d in turn:
                core_copy(p // 2, d).start()
            runs.append(stages(p // 2))
            for run in reversed(runs):
                advance(run)
    live = list(runs)
    while live:
        live = [run for run in live if advance(run)]


def shards(expert_ids, shard_length):
    layers, chosen, slots = expert_ids.shape
    toks = lax.axis_size("tok")
    owners = lax.axis_size("own")
    bits = toks.bit_length() - 2
    share = E // owners // ROWS * COLS
    kept = halvings(bits, share)
    piece = kept[-1][0]
    pieces = share // piece
    pairs = layers - 1
    nslot = pairs // 2
    tile = (ROWS, LANES)
    f32 = jnp.float32
    dma = pltpu.SemaphoreType.DMA
    scratch = [pltpu.VMEM((E, slots), HOT)] * layers
    scratch += [
        pltpu.VMEM((E, E), f32),
        pltpu.VMEM((pairs, owners, share) + tile, f32),
        pltpu.VMEM((nslot, owners, share) + tile, f32),
    ]
    scratch += [pltpu.VMEM((nslot, owners, size) + tile, f32) for size, _ in kept]
    scratch += [
        pltpu.VMEM((nslot, owners, piece) + tile, f32),
        pltpu.VMEM((nslot, owners - 1, piece) + tile, f32),
        pltpu.VMEM((pairs, pieces, piece) + tile, f32),
        pltpu.VMEM((nslot, bits + 1) + tile, f32),
        pltpu.VMEM((nslot, bits) + tile, f32),
        pltpu.VMEM((nslot, owners - 1) + tile, f32),
        pltpu.VMEM((pairs,) + tile, f32),
        dma((2, nslot, owners)),
        dma((2, nslot, bits, owners)),
        dma((2, nslot, owners)),
        dma((2, nslot, 2, pieces)),
        dma((2, nslot, bits)),
        dma((2, nslot, owners)),
    ]
    return pl.pallas_call(
        functools.partial(kernel, bits, owners, kept),
        out_shape=jax.ShapeDtypeStruct((pairs, E // owners, E), f32),
        in_specs=[
            pl.BlockSpec(memory_space=pltpu.SMEM),
            pl.BlockSpec(memory_space=pltpu.VMEM),
        ],
        out_specs=pl.BlockSpec(memory_space=pltpu.VMEM),
        scratch_shapes=scratch,
        compiler_params=pltpu.CompilerParams(
            collective_id=0, has_side_effects=True, vmem_limit_bytes=60 * 2**20
        ),
    )(shard_length, expert_ids)


def solution(mesh):
    placed = (P(None, None, ("tok", "own")), P(("tok", "own")))
    return jax.shard_map(
        shards, mesh=mesh, in_specs=placed, out_specs=P(None, "own", None), check_vma=False
    )
```
